32 devices in a mesh: grid: 16 (over z, y, x), band: 2 (over core).
Axes of the slice: x: 2, y: 2, z: 4, core: 2. Of those that a mesh axis runs over, the one named last changes fastest.
Arguments:
- orbitals: float32 [16, 16, 32, 32, 128], P('grid', 'band'), may hold values from -24 to 24, as said below
- potential: float32 [16, 32, 32, 128], P('grid'), may hold values from -1 to 1
Outputs:
- rotated: float32 [16, 16, 32, 32, 128], P('grid', 'band')
The draws below stay inside these ranges and needn't reach their ends.
Inputs may be any that keep to these rules, and one draw needn't show every extreme that they name: `orbitals`: real-valued orbital samples.
All inputs are finite; a program needn't handle non-finite values.
Results may differ from the reference program's by a relative error of at most 0.00013.
Values sent between devices are 32-bit elements; how exact they have to be, the bound alone decides.
A program may use at most 128 MiB of HBM per device.

```python
import jax
import jax.numpy as jnp
from jax import lax

ORB = 16
RADIUS = 3
CX = 32
CY = 32
CZ = 128
PX = 2
PY = 2
PZ = 4
NX = 64
NY = 64
NZ = 512
NCELLS = 2097152
N_GRID = 16


def draw_orbitals(key, part):
    shape = (N_GRID, ORB, CX, CY, CZ)
    base = jnp.clip(jax.random.normal(key, shape, jnp.float32), -4.0, 4.0)
    mixed = base + 0.5 * jnp.roll(base, 1, axis=1) + 0.25 * jnp.roll(base, 3, axis=1)
    ramp = 1.0 + 2.0 * jnp.arange(N_GRID, dtype=jnp.float32) / max(N_GRID - 1, 1)
    result = mixed * ramp[:, None, None, None, None]
    return result


def level_of(key, shape, pieces, smallest, largest):
    loudness, own = 1.0, jax.random.fold_in(key, 6)
    for dim, parts in pieces:
        heights = jnp.exp(jax.random.uniform(jax.random.fold_in(own, dim), (parts,), jnp.float32, smallest / len(pieces), largest / len(pieces)))
        loudness = loudness * jnp.repeat(heights, shape[dim] // parts).reshape([-1 if axis == dim else 1 for axis in range(len(shape))])
    return loudness


def setup_inputs(seed: int = 0) -> dict:
    splits = jax.random.split(jax.random.key(seed), 3)
    orbitals = draw_orbitals(jax.random.fold_in(splits[2], 71), 0)
    potential = jnp.clip(jax.random.uniform(splits[1], (N_GRID, CX, CY, CZ), jnp.float32, -1.0, 1.0) * level_of(splits[1], (N_GRID, CX, CY, CZ), ((0, 16),), -0.4, 0.0), -1.0, 1.0)
    return {"orbitals": orbitals, "potential": potential}


COEFFS = (-49.0 / 18.0, 1.5, -0.15, 1.0 / 90.0)
CENTER = 5.75
HALF_WIDTH = 4.75

def apply_hamil(values_in, potential_grid):
    padded = jnp.pad(values_in, RADIUS)
    extent = values_in.shape
    summed = 3.0 * COEFFS[0] * values_in
    for dim_index in range(3):
        for reach in range(1, RADIUS + 1):
            upper_start = [RADIUS, RADIUS, RADIUS]
            lower_start = [RADIUS, RADIUS, RADIUS]
            upper_start[dim_index] = RADIUS + reach
            lower_start[dim_index] = RADIUS - reach
            upper_part = lax.dynamic_slice(padded, upper_start, extent)
            lower_part = lax.dynamic_slice(padded, lower_start, extent)
            summed = summed + COEFFS[reach] * (upper_part + lower_part)
    return -0.5 * summed + potential_grid * values_in

def filter_one(values_in, potential_grid):
    first_term = (apply_hamil(values_in, potential_grid) - CENTER * values_in) / HALF_WIDTH
    return 2.0 * (apply_hamil(first_term, potential_grid) - CENTER * first_term) / HALF_WIDTH - values_in

def reference(orbitals, potential):
    grid_orb = orbitals.reshape(PX, PY, PZ, ORB, CX, CY, CZ).transpose(3, 0, 4, 1, 5, 2, 6).reshape(ORB, NX, NY, NZ)
    grid_pot = potential.reshape(PX, PY, PZ, CX, CY, CZ).transpose(0, 3, 1, 4, 2, 5).reshape(NX, NY, NZ)
    filtered = lax.map(lambda single: filter_one(single, grid_pot), grid_orb)
    flat = filtered.reshape(ORB, NCELLS)
    gram = jnp.einsum('ic,jc->ij', flat, flat, precision=lax.Precision.HIGHEST) / NCELLS
    factor = jnp.linalg.cholesky(gram)
    weights = jax.scipy.linalg.solve_triangular(factor, jnp.eye(ORB, dtype=jnp.float32), lower=True)
    rotated = jnp.dot(weights.astype(jnp.float32), flat.astype(jnp.float32), precision=lax.Precision.HIGHEST, preferred_element_type=jnp.float32)
    rotated = rotated.reshape(ORB, PX, CX, PY, CY, PZ, CZ).transpose(1, 3, 5, 0, 2, 4, 6)
    return rotated.reshape(N_GRID, ORB, CX, CY, CZ)
```

```python
import functools

import jax
import jax.numpy as jnp
from jax import lax
from jax.experimental import pallas as pl
from jax.experimental.pallas import tpu as pltpu
from jax.sharding import PartitionSpec as P

COEFFS = (-49.0 / 18.0, 1.5, -0.15, 1.0 / 90.0)
CENTER = 5.75
HALF_WIDTH = 4.75
TAPS = tuple(-0.5 * c / HALF_WIDTH for c in COEFFS)
DIAGONAL = 3.0 * -0.5 * COEFFS[0] - CENTER
REACH = 3
LEAD = 8
UNROLL = 4
SLOT = 8
F32, BF16 = jnp.float32, jnp.bfloat16
HIGHEST = lax.Precision.HIGHEST
MESH = pl.DeviceIdType.MESH


def layout(devices_grid):
    parts_x = max(2, devices_grid // 32)
    return (parts_x, parts_x, devices_grid // (parts_x * parts_x))


def dot(a, b, contract=((1,), (0,)), precision=None):
    return lax.dot_general(a, b, (contract, ((), ())), precision=precision, preferred_element_type=F32)


def split(value):
    high = value.astype(BF16)
    return high, (value - high.astype(F32)).astype(BF16)


def iota(shape, dim):
    return lax.broadcasted_iota(jnp.int32, shape, dim)


def kernel(parts, volume, x_hbm, v_hbm, out_hbm, xp, yp, y2, rem, pot, ypack, yrecv, zpack, zrecv, zcorr,
           high, low, acc, place, buf_x, buf_y, buf_z, part, outv,
           load_sem, send_sem, recv_sem, y2_send, y2_recv, oo_send, oo_recv, ar_send, ar_recv, out_sem):
    count, cx, cy, cz = y2.shape
    nx, ny, nz = parts
    sizes = (nx, ny, nz)
    strides = (ny * nz, nz, 1)
    grid_index = lax.axis_index("grid")
    band = lax.axis_index("band")
    pos = (grid_index // (ny * nz), grid_index // nz % ny, grid_index % nz)
    rows = count * cy
    tiles = cy // 8
    per_pack = cz // SLOT

    def loads(o):
        return pltpu.make_async_copy(
            x_hbm.at[0, o], xp.at[o, REACH:REACH + cx, LEAD:LEAD + cy], load_sem.at[o])

    pot_load = pltpu.make_async_copy(v_hbm.at[0], pot, load_sem.at[count])
    pot_load.start()

    @pl.loop(0, count)
    def _(o):
        loads(o).start()

    barrier = pltpu.get_barrier_semaphore()

    def line_peer(dim, k):
        return grid_index + (lax.rem(pos[dim] + k, sizes[dim]) - pos[dim]) * strides[dim]

    for dim in range(3):
        for k in range(1, sizes[dim]):
            pl.semaphore_signal(barrier, inc=1, device_id={"grid": line_peer(dim, k)}, device_id_type=MESH)
    pl.semaphore_signal(barrier, inc=1, device_id={"band": 1 - band}, device_id_type=MESH)
    pl.semaphore_wait(barrier, nx + ny + nz - 2)

    can_send = []
    for dim in range(3):
        can_send += [pos[dim] < sizes[dim] - 1, pos[dim] > 0]
    can_recv = [can_send[1], can_send[0], can_send[3], can_send[2], can_send[5], can_send[4]]

    def face(stage, o, d):
        field = (xp, yp)[stage]
        if d == 0:
            src, dst = field.at[o, cx:cx + REACH, LEAD:LEAD + cy], field.at[o, 0:REACH, LEAD:LEAD + cy]
        elif d == 1:
            src = field.at[o, REACH:2 * REACH, LEAD:LEAD + cy]
            dst = field.at[o, cx + REACH:cx + 2 * REACH, LEAD:LEAD + cy]
        elif d < 4:
            src, dst = ypack.at[stage, o, d - 2], yrecv.at[stage, o, d - 2]
        else:
            src, dst = zpack.at[stage, o], zrecv.at[stage, o, d - 4]
        step = strides[d // 2] * (1 - 2 * (d % 2))
        return pltpu.make_async_remote_copy(
            src_ref=src, dst_ref=dst, send_sem=send_sem.at[stage, o, d], recv_sem=recv_sem.at[stage, o, d],
            device_id={"grid": grid_index + step}, device_id_type=MESH)

    for d in range(6):
        @pl.when(jnp.logical_not(can_recv[d]))
        def _(d=d):
            @pl.loop(0, 2 * count)
            def _(i):
                stage, o = i // count, i % count
                if d < 2:
                    start = (0, cx + REACH)[d]
                    for k in range(REACH):
                        zero = jnp.zeros((cy, cz), F32)

                        @pl.when(stage == 0)
                        def _():
                            xp[o, start + k, LEAD:LEAD + cy, :] = zero

                        @pl.when(stage == 1)
                        def _():
                            yp[o, start + k, LEAD:LEAD + cy, :] = zero
                elif d < 4:
                    yrecv[stage, o, d - 2] = jnp.zeros(yrecv.shape[3:], F32)
                else:
                    zrecv[stage, o, d - 4] = jnp.zeros(zrecv.shape[3:], F32)

    def pack_y(stage, field, o):
        for x in range(cx):
            ypack[stage, o, 0, REACH * x:REACH * (x + 1), :] = field[o, REACH + x, LEAD + cy - REACH:LEAD + cy, :]
            ypack[stage, o, 1, REACH * x:REACH * (x + 1), :] = field[o, REACH + x, LEAD:LEAD + REACH, :]

    def unpack_y(stage, field, o):
        for x in range(cx):
            field[o, REACH + x, LEAD - REACH:LEAD, :] = yrecv[stage, o, 0, REACH * x:REACH * (x + 1), :]
            field[o, REACH + x, LEAD + cy:LEAD + cy + REACH, :] = yrecv[stage, o, 1, REACH * x:REACH * (x + 1), :]

    lane = iota((8, cz), 1)
    lane_slot = lane // SLOT

    def pack_z_tile(stage, o, x0, y0, values):
        group, slot = x0 // per_pack, x0 % per_pack
        packed = zpack[stage, o, group, pl.ds(y0, 8), :]
        for u, value in enumerate(values):
            turned = pltpu.roll(value, (slot + u) * SLOT + REACH, 1)
            packed = jnp.where(lane_slot == slot + u, turned, packed)
        zpack[stage, o, group, pl.ds(y0, 8), :] = packed

    def correct_z(stage, o):
        own = zpack[stage, o]
        lanes = iota(own.shape, 2) % SLOT
        from_left = jnp.where(lanes < REACH, zrecv[stage, o, 0] - own, 0.0).reshape(-1, cz)
        right = (lanes >= REACH) & (lanes < 2 * REACH)
        from_right = jnp.where(right, zrecv[stage, o, 1] - own, 0.0).reshape(-1, cz)
        low_side, high_side = 0.0, 0.0
        for r in range(1, REACH + 1):
            low_side = low_side + TAPS[r] * pltpu.roll(from_left, r, 1)
            high_side = high_side + TAPS[r] * pltpu.roll(from_right, cz - r, 1)
        low_side, high_side = low_side.reshape(own.shape), high_side.reshape(own.shape)
        zcorr[...] = jnp.where(lanes < REACH, high_side, jnp.where(right, low_side, 0.0))

    edge = (lane < REACH) | (lane >= cz - REACH)

    def stencil_tile(field, o, x0, t):
        y0 = 8 * t
        window = [field[o, x0 + i, LEAD + y0:LEAD + y0 + 8, :] for i in range(UNROLL + 2 * REACH)]
        results = []
        group, slot = x0 // per_pack, x0 % per_pack
        corr = zcorr[group, y0:y0 + 8, :]
        for u in range(UNROLL):
            center = window[u + REACH]
            total = pot[x0 + u, y0:y0 + 8, :] * center
            for r in range(1, REACH + 1):
                pair = window[u + REACH + r] + window[u + REACH - r]
                up = field[o, x0 + u + REACH, LEAD + y0 + r:LEAD + y0 + r + 8, :]
                down = field[o, x0 + u + REACH, LEAD + y0 - r:LEAD + y0 - r + 8, :]
                turned = pltpu.roll(center, r, 1) + pltpu.roll(center, cz - r, 1)
                total = total + TAPS[r] * ((pair + turned) + (up + down))
            fix = pltpu.roll(corr, cz - (slot + u) * SLOT - REACH, 1)
            results.append(total + jnp.where(edge, fix, 0.0))
        return results

    def start_faces(stage, o):
        for d in range(6):
            @pl.when(can_send[d])
            def _(d=d):
                face(stage, o, d).start()

    def wait_faces(stage, o):
        for d in range(6):
            @pl.when(can_recv[d])
            def _(d=d):
                face(stage, o, d).wait_recv()

    @pl.loop(0, count)
    def _(o):
        loads(o).wait()
        pack_y(0, xp, o)

        @pl.loop(0, cx // UNROLL)
        def _(g):
            x0 = g * UNROLL
            for t in range(tiles):
                pack_z_tile(0, o, x0, 8 * t,
                            [xp[o, x0 + u + REACH, LEAD + 8 * t:LEAD + 8 * t + 8, :] for u in range(UNROLL)])

        start_faces(0, o)

    pot_load.wait()

    @pl.loop(0, cx)
    def _(x):
        pot[x] = (pot[x] + DIAGONAL) * (1.0 / HALF_WIDTH)

    @pl.loop(0, count)
    def _(o):
        wait_faces(0, o)
        unpack_y(0, xp, o)
        correct_z(0, o)

        @pl.loop(0, cx // UNROLL)
        def _(g):
            x0 = g * UNROLL
            for t in range(tiles):
                values = stencil_tile(xp, o, x0, t)
                for u in range(UNROLL):
                    yp[o, x0 + u + REACH, LEAD + 8 * t:LEAD + 8 * t + 8, :] = values[u]
                pack_z_tile(1, o, x0, 8 * t, values)

        pack_y(1, yp, o)
        start_faces(1, o)

    def hand_over(o):
        return pltpu.make_async_remote_copy(
            src_ref=y2.at[o], dst_ref=rem.at[o], send_sem=y2_send.at[o], recv_sem=y2_recv.at[o],
            device_id={"band": 1 - band}, device_id_type=MESH)

    @pl.loop(0, count)
    def _(o):
        wait_faces(1, o)
        unpack_y(1, yp, o)
        correct_z(1, o)

        @pl.loop(0, cx // UNROLL)
        def _(g):
            x0 = g * UNROLL
            for t in range(tiles):
                values = stencil_tile(yp, o, x0, t)
                for u in range(UNROLL):
                    start = xp[o, x0 + u + REACH, LEAD + 8 * t:LEAD + 8 * t + 8, :]
                    y2[o, x0 + u, 8 * t:8 * t + 8, :] = (values[u] + values[u]) - start

        hand_over(o).start()

    def wide(ref, x0):
        return jnp.concatenate([ref[:, x0 + u].reshape(rows, cz) for u in range(UNROLL)], axis=1)

    def split_block(which, field, x0):
        for u in range(UNROLL):
            high[which, :, x0 + u], low[which, :, x0 + u] = split(field[:, x0 + u])

    def gram(which):
        acc[...] = jnp.zeros_like(acc)

        @pl.loop(0, cx // UNROLL)
        def _(g):
            x0 = g * UNROLL
            split_block(which, (y2, rem)[which], x0)
            left_high, left_low = wide(high.at[0], x0), wide(low.at[0], x0)
            right_high, right_low = wide(high.at[which], x0), wide(low.at[which], x0)
            inner = ((1,), (1,))
            acc[...] += (dot(left_high, right_high, inner) + dot(left_high, right_low, inner)
                         + dot(left_low, right_high, inner))

    same_y = (iota((rows, rows), 0) % cy) == (iota((rows, rows), 1) % cy)

    def row_pick(which):
        own = jnp.where(which == 0, band, 1 - band) * count
        return (iota((2 * count, rows), 0) == iota((2 * count, rows), 1) // cy + own).astype(F32)

    def column_pick(which):
        own = jnp.where(which == 0, band, 1 - band) * count
        return (iota((rows, cz), 1) == iota((rows, cz), 0) // cy + own).astype(F32)

    gram(0)
    masked = jnp.where(same_y, acc[...], 0.0)
    place[0] = dot(dot(row_pick(0), masked, precision=HIGHEST), column_pick(0), precision=HIGHEST)
    oo_copy = pltpu.make_async_remote_copy(
        src_ref=place.at[0], dst_ref=place.at[1], send_sem=oo_send, recv_sem=oo_recv,
        device_id={"band": 1 - band}, device_id_type=MESH)
    oo_copy.start()

    @pl.loop(0, count)
    def _(o):
        hand_over(o).wait_recv()

    gram(1)
    masked = jnp.where(same_y, acc[...], 0.0)
    cross = dot(dot(row_pick(0), masked, precision=HIGHEST), column_pick(1), precision=HIGHEST)
    flipped = dot(dot(row_pick(1), masked, ((1,), (1,)), HIGHEST), column_pick(0), precision=HIGHEST)
    oo_copy.wait_recv()
    total = place[0] + place[1] + cross + flipped

    buffers = (buf_x, buf_y, buf_z)

    def reduce_copy(dim, k):
        return pltpu.make_async_remote_copy(
            src_ref=part.at[dim], dst_ref=buffers[dim].at[pos[dim]],
            send_sem=ar_send.at[dim, k], recv_sem=ar_recv.at[dim, k],
            device_id={"grid": line_peer(dim, k)}, device_id_type=MESH)

    for dim in (2, 1, 0):
        part[dim] = total
        buffers[dim][pos[dim]] = total
        for k in range(1, sizes[dim]):
            reduce_copy(dim, k).start()
        for k in range(1, sizes[dim]):
            reduce_copy(dim, k).wait_recv()
        total = buffers[dim][0]
        for k in range(1, sizes[dim]):
            total = total + buffers[dim][k]

    orbs = 2 * count
    row_id, lane_id = iota((orbs, cz), 0), iota((orbs, cz), 1)
    work = jnp.where(lane_id < orbs, total * (1.0 / volume), (lane_id == row_id + orbs).astype(F32))
    for k in range(orbs):
        scale = 1.0 / jnp.sqrt(work[k:k + 1, k:k + 1])
        pivot = work[k:k + 1, :] * scale
        column = jnp.where(row_id > k, work[:, k:k + 1] * scale, 0.0)
        work = jnp.where(row_id == k, pivot, work - column * pivot)

    def spread(which):
        own = jnp.where(which == 0, band, 1 - band) * count
        rows_pick = (iota((rows, orbs), 1) == iota((rows, orbs), 0) // cy + band * count).astype(F32)
        lanes_pick = (iota((cz, rows), 0) == iota((cz, rows), 1) // cy + own + orbs).astype(F32)
        full = dot(dot(rows_pick, work, precision=HIGHEST), lanes_pick, precision=HIGHEST)
        return split(jnp.where(same_y, full, 0.0))

    own_high, own_low = spread(0)
    far_high, far_low = spread(1)

    def store(x0):
        return pltpu.make_async_copy(
            outv.at[:, pl.ds(x0, UNROLL)], out_hbm.at[0, :, pl.ds(x0, UNROLL)], out_sem.at[x0 // UNROLL])

    @pl.loop(0, cx // UNROLL)
    def _(g):
        x0 = g * UNROLL
        a_high, a_low = wide(high.at[0], x0), wide(low.at[0], x0)
        b_high, b_low = wide(high.at[1], x0), wide(low.at[1], x0)
        result = (dot(own_high, a_high) + dot(own_high, a_low) + dot(own_low, a_high)
                  + dot(far_high, b_high) + dot(far_high, b_low) + dot(far_low, b_high))
        for u in range(UNROLL):
            outv[:, x0 + u] = result[:, u * cz:(u + 1) * cz].reshape(count, cy, cz)
        store(x0).start()

    @pl.loop(0, cx // UNROLL)
    def _(g):
        store(g * UNROLL).wait()

    @pl.loop(0, count)
    def _(o):
        for stage in range(2):
            for d in range(6):
                @pl.when(can_send[d])
                def _(stage=stage, d=d):
                    face(stage, o, d).wait_send()
        hand_over(o).wait_send()

    oo_copy.wait_send()
    for dim in range(3):
        for k in range(1, sizes[dim]):
            reduce_copy(dim, k).wait_send()


def on_device(orbitals, potential):
    _, count, cx, cy, cz = orbitals.shape
    devices_grid = lax.axis_size("grid")
    parts = layout(devices_grid)
    volume = cx * cy * cz * devices_grid
    rows, orbs = count * cy, 2 * count
    groups = cx * SLOT // cz
    padded = (count, cx + 2 * REACH, cy + 2 * LEAD, cz)
    block = (count, cx, cy, cz)
    dma = pltpu.SemaphoreType.DMA
    most = max(parts)
    any_spec = pl.BlockSpec(memory_space=pl.ANY)
    return pl.pallas_call(
        functools.partial(kernel, parts, volume),
        out_shape=jax.ShapeDtypeStruct(orbitals.shape, F32),
        in_specs=[any_spec, any_spec],
        out_specs=any_spec,
        scratch_shapes=[
            pltpu.VMEM(padded, F32), pltpu.VMEM(padded, F32),
            pltpu.VMEM(block, F32), pltpu.VMEM(block, F32), pltpu.VMEM((cx, cy, cz), F32),
            pltpu.VMEM((2, count, 2, REACH * cx, cz), F32), pltpu.VMEM((2, count, 2, REACH * cx, cz), F32),
            pltpu.VMEM((2, count, groups, cy, cz), F32), pltpu.VMEM((2, count, 2, groups, cy, cz), F32),
            pltpu.VMEM((groups, cy, cz), F32),
            pltpu.VMEM((2,) + block, BF16), pltpu.VMEM((2,) + block, BF16),
            pltpu.VMEM((rows, rows), F32), pltpu.VMEM((2, orbs, cz), F32),
            pltpu.VMEM((parts[0], orbs, cz), F32), pltpu.VMEM((parts[1], orbs, cz), F32),
            pltpu.VMEM((parts[2], orbs, cz), F32), pltpu.VMEM((3, orbs, cz), F32),
            pltpu.VMEM(block, F32),
            dma((count + 1,)), dma((2, count, 6)), dma((2, count, 6)), dma((count,)), dma((count,)),
            dma, dma, dma((3, most)), dma((3, most)), dma((cx // UNROLL,)),
        ],
        compiler_params=pltpu.CompilerParams(
            collective_id=0, has_side_effects=True, vmem_limit_bytes=60 * 1024 * 1024),
    )(orbitals, potential)


def solution(mesh):
    in_specs = (P("grid", "band", None, None, None), P("grid", None, None, None))
    out_specs = P("grid", "band", None, None, None)
    return jax.shard_map(
        on_device, mesh=mesh, in_specs=in_specs, out_specs=out_specs, check_vma=False
    )
```

```python
import functools

import jax
import jax.numpy as jnp
from jax import lax
from jax.experimental import pallas as pl
from jax.experimental.pallas import tpu as pltpu
from jax.sharding import PartitionSpec as P

COEFFS = (-49.0 / 18.0, 1.5, -0.15, 1.0 / 90.0)
CENTER = 5.75
HALF_WIDTH = 4.75
TAPS = tuple(-0.5 * c / HALF_WIDTH for c in COEFFS)
DIAGONAL = 3.0 * -0.5 * COEFFS[0] - CENTER
REACH = 3
LEAD = 8
UNROLL = 4
SLOT = 8
F32, BF16 = jnp.float32, jnp.bfloat16
HIGHEST = lax.Precision.HIGHEST
MESH = pl.DeviceIdType.MESH


def layout(devices_grid):
    parts_x = max(2, devices_grid // 32)
    return (parts_x, parts_x, devices_grid // (parts_x * parts_x))


def dot(a, b, contract=((1,), (0,)), precision=None):
    return lax.dot_general(a, b, (contract, ((), ())), precision=precision, preferred_element_type=F32)


def split(value):
    high = value.astype(BF16)
    return high, (value - high.astype(F32)).astype(BF16)


def iota(shape, dim):
    return lax.broadcasted_iota(jnp.int32, shape, dim)


def kernel(parts, volume, x_hbm, v_hbm, out_hbm, xp, yp, y2, rem, pot, ypack, yrecv, zpack, zrecv, zcorr,
           high, low, acc, place, sums, outv,
           load_sem, send_sem, recv_sem, y2_send, y2_recv, oo_send, oo_recv, ar_send, ar_recv, out_sem):
    count, cx, cy, cz = y2.shape
    nx, ny, nz = parts
    sizes = (nx, ny, nz)
    devices_grid = nx * ny * nz
    strides = (ny * nz, nz, 1)
    grid_index = lax.axis_index("grid")
    band = lax.axis_index("band")
    pos = (grid_index // (ny * nz), grid_index // nz % ny, grid_index % nz)
    rows = count * cy
    tiles = cy // 8
    per_pack = cz // SLOT

    def loads(o):
        return pltpu.make_async_copy(
            x_hbm.at[0, o], xp.at[o, REACH:REACH + cx, LEAD:LEAD + cy], load_sem.at[o])

    pot_load = pltpu.make_async_copy(v_hbm.at[0], pot, load_sem.at[count])
    pot_load.start()

    @pl.loop(0, count)
    def _(o):
        loads(o).start()

    barrier = pltpu.get_barrier_semaphore()

    def grid_peer(k):
        return lax.rem(grid_index + k, devices_grid)

    @pl.loop(1, devices_grid)
    def _(k):
        pl.semaphore_signal(barrier, inc=1, device_id={"grid": grid_peer(k)}, device_id_type=MESH)

    pl.semaphore_signal(barrier, inc=1, device_id={"band": 1 - band}, device_id_type=MESH)
    pl.semaphore_wait(barrier, devices_grid)

    can_send = []
    for dim in range(3):
        can_send += [pos[dim] < sizes[dim] - 1, pos[dim] > 0]
    can_recv = [can_send[1], can_send[0], can_send[3], can_send[2], can_send[5], can_send[4]]

    def face(stage, o, d):
        field = (xp, yp)[stage]
        if d == 0:
            src, dst = field.at[o, cx:cx + REACH, LEAD:LEAD + cy], field.at[o, 0:REACH, LEAD:LEAD + cy]
        elif d == 1:
            src = field.at[o, REACH:2 * REACH, LEAD:LEAD + cy]
            dst = field.at[o, cx + REACH:cx + 2 * REACH, LEAD:LEAD + cy]
        elif d < 4:
            src, dst = ypack.at[stage, o, d - 2], yrecv.at[stage, o, d - 2]
        else:
            src, dst = zpack.at[stage, o], zrecv.at[stage, o, d - 4]
        step = strides[d // 2] * (1 - 2 * (d % 2))
        return pltpu.make_async_remote_copy(
            src_ref=src, dst_ref=dst, send_sem=send_sem.at[stage, o, d], recv_sem=recv_sem.at[stage, o, d],
            device_id={"grid": grid_index + step}, device_id_type=MESH)

    for d in range(6):
        @pl.when(jnp.logical_not(can_recv[d]))
        def _(d=d):
            @pl.loop(0, 2 * count)
            def _(i):
                stage, o = i // count, i % count
                if d < 2:
                    start = (0, cx + REACH)[d]
                    for k in range(REACH):
                        zero = jnp.zeros((cy, cz), F32)

                        @pl.when(stage == 0)
                        def _():
                            xp[o, start + k, LEAD:LEAD + cy, :] = zero

                        @pl.when(stage == 1)
                        def _():
                            yp[o, start + k, LEAD:LEAD + cy, :] = zero
                elif d < 4:
                    yrecv[stage, o, d - 2] = jnp.zeros(yrecv.shape[3:], F32)
                else:
                    zrecv[stage, o, d - 4] = jnp.zeros(zrecv.shape[3:], F32)

    def pack_y(stage, field, o):
        for x in range(cx):
            ypack[stage, o, 0, REACH * x:REACH * (x + 1), :] = field[o, REACH + x, LEAD + cy - REACH:LEAD + cy, :]
            ypack[stage, o, 1, REACH * x:REACH * (x + 1), :] = field[o, REACH + x, LEAD:LEAD + REACH, :]

    def unpack_y(stage, field, o):
        for x in range(cx):
            field[o, REACH + x, LEAD - REACH:LEAD, :] = yrecv[stage, o, 0, REACH * x:REACH * (x + 1), :]
            field[o, REACH + x, LEAD + cy:LEAD + cy + REACH, :] = yrecv[stage, o, 1, REACH * x:REACH * (x + 1), :]

    lane = iota((8, cz), 1)
    lane_slot = lane // SLOT

    def pack_z_tile(stage, o, x0, y0, values):
        group, slot = x0 // per_pack, x0 % per_pack
        packed = zpack[stage, o, group, pl.ds(y0, 8), :]
        for u, value in enumerate(values):
            turned = pltpu.roll(value, (slot + u) * SLOT + REACH, 1)
            packed = jnp.where(lane_slot == slot + u, turned, packed)
        zpack[stage, o, group, pl.ds(y0, 8), :] = packed

    def correct_z(stage, o):
        own = zpack[stage, o]
        lanes = iota(own.shape, 2) % SLOT
        from_left = jnp.where(lanes < REACH, zrecv[stage, o, 0] - own, 0.0).reshape(-1, cz)
        right = (lanes >= REACH) & (lanes < 2 * REACH)
        from_right = jnp.where(right, zrecv[stage, o, 1] - own, 0.0).reshape(-1, cz)
        low_side, high_side = 0.0, 0.0
        for r in range(1, REACH + 1):
            low_side = low_side + TAPS[r] * pltpu.roll(from_left, r, 1)
            high_side = high_side + TAPS[r] * pltpu.roll(from_right, cz - r, 1)
        low_side, high_side = low_side.reshape(own.shape), high_side.reshape(own.shape)
        zcorr[...] = jnp.where(lanes < REACH, high_side, jnp.where(right, low_side, 0.0))

    edge = (lane < REACH) | (lane >= cz - REACH)

    def stencil_tile(field, o, x0, t):
        y0 = 8 * t
        window = [field[o, x0 + i, LEAD + y0:LEAD + y0 + 8, :] for i in range(UNROLL + 2 * REACH)]
        results = []
        group, slot = x0 // per_pack, x0 % per_pack
        corr = zcorr[group, y0:y0 + 8, :]
        for u in range(UNROLL):
            center = window[u + REACH]
            total = pot[x0 + u, y0:y0 + 8, :] * center
            for r in range(1, REACH + 1):
                pair = window[u + REACH + r] + window[u + REACH - r]
                up = field[o, x0 + u + REACH, LEAD + y0 + r:LEAD + y0 + r + 8, :]
                down = field[o, x0 + u + REACH, LEAD + y0 - r:LEAD + y0 - r + 8, :]
                turned = pltpu.roll(center, r, 1) + pltpu.roll(center, cz - r, 1)
                total = total + TAPS[r] * ((pair + turned) + (up + down))
            fix = pltpu.roll(corr, cz - (slot + u) * SLOT - REACH, 1)
            results.append(total + jnp.where(edge, fix, 0.0))
        return results

    def start_faces(stage, o):
        for d in range(6):
            @pl.when(can_send[d])
            def _(d=d):
                face(stage, o, d).start()

    def wait_faces(stage, o):
        for d in range(6):
            @pl.when(can_recv[d])
            def _(d=d):
                face(stage, o, d).wait_recv()

    @pl.loop(0, count)
    def _(o):
        loads(o).wait()
        pack_y(0, xp, o)

        @pl.loop(0, cx // UNROLL)
        def _(g):
            x0 = g * UNROLL
            for t in range(tiles):
                pack_z_tile(0, o, x0, 8 * t,
                            [xp[o, x0 + u + REACH, LEAD + 8 * t:LEAD + 8 * t + 8, :] for u in range(UNROLL)])

        start_faces(0, o)

    pot_load.wait()

    @pl.loop(0, cx)
    def _(x):
        pot[x] = (pot[x] + DIAGONAL) * (1.0 / HALF_WIDTH)

    @pl.loop(0, count)
    def _(o):
        wait_faces(0, o)
        unpack_y(0, xp, o)
        correct_z(0, o)

        @pl.loop(0, cx // UNROLL)
        def _(g):
            x0 = g * UNROLL
            for t in range(tiles):
                values = stencil_tile(xp, o, x0, t)
                for u in range(UNROLL):
                    yp[o, x0 + u + REACH, LEAD + 8 * t:LEAD + 8 * t + 8, :] = values[u]
                pack_z_tile(1, o, x0, 8 * t, values)

        pack_y(1, yp, o)
        start_faces(1, o)

    def hand_over(o):
        return pltpu.make_async_remote_copy(
            src_ref=y2.at[o], dst_ref=rem.at[o], send_sem=y2_send.at[o], recv_sem=y2_recv.at[o],
            device_id={"band": 1 - band}, device_id_type=MESH)

    @pl.loop(0, count)
    def _(o):
        wait_faces(1, o)
        unpack_y(1, yp, o)
        correct_z(1, o)

        @pl.loop(0, cx // UNROLL)
        def _(g):
            x0 = g * UNROLL
            for t in range(tiles):
                values = stencil_tile(yp, o, x0, t)
                for u in range(UNROLL):
                    start = xp[o, x0 + u + REACH, LEAD + 8 * t:LEAD + 8 * t + 8, :]
                    y2[o, x0 + u, 8 * t:8 * t + 8, :] = (values[u] + values[u]) - start

        hand_over(o).start()

    def wide(ref, x0):
        return jnp.concatenate([ref[:, x0 + u].reshape(rows, cz) for u in range(UNROLL)], axis=1)

    def split_block(which, field, x0):
        for u in range(UNROLL):
            high[which, :, x0 + u], low[which, :, x0 + u] = split(field[:, x0 + u])

    def gram(which):
        acc[...] = jnp.zeros_like(acc)

        @pl.loop(0, cx // UNROLL)
        def _(g):
            x0 = g * UNROLL
            split_block(which, (y2, rem)[which], x0)
            left_high, left_low = wide(high.at[0], x0), wide(low.at[0], x0)
            right_high, right_low = wide(high.at[which], x0), wide(low.at[which], x0)
            inner = ((1,), (1,))
            acc[...] += (dot(left_high, right_high, inner) + dot(left_high, right_low, inner)
                         + dot(left_low, right_high, inner))

    same_y = (iota((rows, rows), 0) % cy) == (iota((rows, rows), 1) % cy)

    def row_pick(which):
        own = jnp.where(which == 0, band, 1 - band) * count
        return (iota((2 * count, rows), 0) == iota((2 * count, rows), 1) // cy + own).astype(F32)

    def column_pick(which):
        own = jnp.where(which == 0, band, 1 - band) * count
        return (iota((rows, cz), 1) == iota((rows, cz), 0) // cy + own).astype(F32)

    gram(0)
    masked = jnp.where(same_y, acc[...], 0.0)
    place[0] = dot(dot(row_pick(0), masked, precision=HIGHEST), column_pick(0), precision=HIGHEST)
    oo_copy = pltpu.make_async_remote_copy(
        src_ref=place.at[0], dst_ref=place.at[1], send_sem=oo_send, recv_sem=oo_recv,
        device_id={"band": 1 - band}, device_id_type=MESH)
    oo_copy.start()

    @pl.loop(0, count)
    def _(o):
        hand_over(o).wait_recv()

    gram(1)
    masked = jnp.where(same_y, acc[...], 0.0)
    cross = dot(dot(row_pick(0), masked, precision=HIGHEST), column_pick(1), precision=HIGHEST)
    flipped = dot(dot(row_pick(1), masked, ((1,), (1,)), HIGHEST), column_pick(0), precision=HIGHEST)
    oo_copy.wait_recv()
    total = place[0] + place[1] + cross + flipped

    sums[grid_index] = total

    def reduce_copy(k):
        return pltpu.make_async_remote_copy(
            src_ref=sums.at[grid_index], dst_ref=sums.at[grid_index],
            send_sem=ar_send.at[k], recv_sem=ar_recv.at[k],
            device_id={"grid": grid_peer(k)}, device_id_type=MESH)

    @pl.loop(1, devices_grid)
    def _(k):
        reduce_copy(k).start()

    @pl.loop(1, devices_grid)
    def _(k):
        reduce_copy(k).wait_recv()

    total = sums[0]
    for k in range(1, devices_grid):
        total = total + sums[k]

    orbs = 2 * count
    row_id, lane_id = iota((orbs, cz), 0), iota((orbs, cz), 1)
    work = jnp.where(lane_id < orbs, total * (1.0 / volume), (lane_id == row_id + orbs).astype(F32))
    for k in range(orbs):
        scale = 1.0 / jnp.sqrt(work[k:k + 1, k:k + 1])
        pivot = work[k:k + 1, :] * scale
        column = jnp.where(row_id > k, work[:, k:k + 1] * scale, 0.0)
        work = jnp.where(row_id == k, pivot, work - column * pivot)

    def spread(which):
        own = jnp.where(which == 0, band, 1 - band) * count
        rows_pick = (iota((rows, orbs), 1) == iota((rows, orbs), 0) // cy + band * count).astype(F32)
        lanes_pick = (iota((cz, rows), 0) == iota((cz, rows), 1) // cy + own + orbs).astype(F32)
        full = dot(dot(rows_pick, work, precision=HIGHEST), lanes_pick, precision=HIGHEST)
        return split(jnp.where(same_y, full, 0.0))

    own_high, own_low = spread(0)
    far_high, far_low = spread(1)

    def store(x0):
        return pltpu.make_async_copy(
            outv.at[:, pl.ds(x0, UNROLL)], out_hbm.at[0, :, pl.ds(x0, UNROLL)], out_sem.at[x0 // UNROLL])

    @pl.loop(0, cx // UNROLL)
    def _(g):
        x0 = g * UNROLL
        a_high, a_low = wide(high.at[0], x0), wide(low.at[0], x0)
        b_high, b_low = wide(high.at[1], x0), wide(low.at[1], x0)
        result = (dot(own_high, a_high) + dot(own_high, a_low) + dot(own_low, a_high)
                  + dot(far_high, b_high) + dot(far_high, b_low) + dot(far_low, b_high))
        for u in range(UNROLL):
            outv[:, x0 + u] = result[:, u * cz:(u + 1) * cz].reshape(count, cy, cz)
        store(x0).start()

    @pl.loop(0, cx // UNROLL)
    def _(g):
        store(g * UNROLL).wait()

    @pl.loop(0, count)
    def _(o):
        for stage in range(2):
            for d in range(6):
                @pl.when(can_send[d])
                def _(stage=stage, d=d):
                    face(stage, o, d).wait_send()
        hand_over(o).wait_send()

    oo_copy.wait_send()

    @pl.loop(1, devices_grid)
    def _(k):
        reduce_copy(k).wait_send()


def on_device(orbitals, potential):
    _, count, cx, cy, cz = orbitals.shape
    devices_grid = lax.axis_size("grid")
    parts = layout(devices_grid)
    volume = cx * cy * cz * devices_grid
    rows, orbs = count * cy, 2 * count
    groups = cx * SLOT // cz
    padded = (count, cx + 2 * REACH, cy + 2 * LEAD, cz)
    block = (count, cx, cy, cz)
    dma = pltpu.SemaphoreType.DMA
    any_spec = pl.BlockSpec(memory_space=pl.ANY)
    return pl.pallas_call(
        functools.partial(kernel, parts, volume),
        out_shape=jax.ShapeDtypeStruct(orbitals.shape, F32),
        in_specs=[any_spec, any_spec],
        out_specs=any_spec,
        scratch_shapes=[
            pltpu.VMEM(padded, F32), pltpu.VMEM(padded, F32),
            pltpu.VMEM(block, F32), pltpu.VMEM(block, F32), pltpu.VMEM((cx, cy, cz), F32),
            pltpu.VMEM((2, count, 2, REACH * cx, cz), F32), pltpu.VMEM((2, count, 2, REACH * cx, cz), F32),
            pltpu.VMEM((2, count, groups, cy, cz), F32), pltpu.VMEM((2, count, 2, groups, cy, cz), F32),
            pltpu.VMEM((groups, cy, cz), F32),
            pltpu.VMEM((2,) + block, BF16), pltpu.VMEM((2,) + block, BF16),
            pltpu.VMEM((rows, rows), F32), pltpu.VMEM((2, orbs, cz), F32),
            pltpu.VMEM((devices_grid, orbs, cz), F32),
            pltpu.VMEM(block, F32),
            dma((count + 1,)), dma((2, count, 6)), dma((2, count, 6)), dma((count,)), dma((count,)),
            dma, dma, dma((devices_grid,)), dma((devices_grid,)), dma((cx // UNROLL,)),
        ],
        compiler_params=pltpu.CompilerParams(
            collective_id=0, has_side_effects=True, vmem_limit_bytes=60 * 1024 * 1024),
    )(orbitals, potential)


def solution(mesh):
    in_specs = (P("grid", "band", None, None, None), P("grid", None, None, None))
    out_specs = P("grid", "band", None, None, None)
    return jax.shard_map(
        on_device, mesh=mesh, in_specs=in_specs, out_specs=out_specs, check_vma=False
    )
```

```python
import functools

import jax
import jax.numpy as jnp
from jax import lax
from jax.experimental import pallas as pl
from jax.experimental.pallas import tpu as pltpu
from jax.sharding import PartitionSpec as P

COEFFS = (-49.0 / 18.0, 1.5, -0.15, 1.0 / 90.0)
CENTER = 5.75
HALF_WIDTH = 4.75
TAPS = tuple(-0.5 * c / HALF_WIDTH for c in COEFFS)
DIAGONAL = 3.0 * -0.5 * COEFFS[0] - CENTER
REACH = 3
LEAD = 8
UNROLL = 4
SLOT = 8
F32, BF16 = jnp.float32, jnp.bfloat16
HIGHEST = lax.Precision.HIGHEST
MESH = pl.DeviceIdType.MESH


def layout(devices_grid):
    parts_x = max(2, devices_grid // 32)
    return (parts_x, parts_x, devices_grid // (parts_x * parts_x))


def dot(a, b, contract=((1,), (0,)), precision=None):
    return lax.dot_general(a, b, (contract, ((), ())), precision=precision, preferred_element_type=F32)


def split(value):
    high = value.astype(BF16)
    return high, (value - high.astype(F32)).astype(BF16)


def iota(shape, dim):
    return lax.broadcasted_iota(jnp.int32, shape, dim)


def kernel(parts, volume, x_hbm, v_hbm, out_hbm, xp, yp, y2, rem, pot, ypack, yrecv, zpack, zrecv, zcorr,
           high, low, acc, place, sums, band_z, outv,
           load_sem, send_sem, recv_sem, y2_send, y2_recv, oo_send, oo_recv, ar_send, ar_recv, out_sem):
    count, cx, cy, cz = y2.shape
    nx, ny, nz = parts
    sizes = (nx, ny, nz)
    devices_grid = nx * ny * nz
    strides = (ny * nz, nz, 1)
    grid_index = lax.axis_index("grid")
    band = lax.axis_index("band")
    pos = (grid_index // (ny * nz), grid_index // nz % ny, grid_index % nz)
    rows = count * cy
    tiles = cy // 8
    per_pack = cz // SLOT

    def loads(o):
        return pltpu.make_async_copy(
            x_hbm.at[0, o], xp.at[o, REACH:REACH + cx, LEAD:LEAD + cy], load_sem.at[o])

    pot_load = pltpu.make_async_copy(v_hbm.at[0], pot, load_sem.at[count])
    pot_load.start()

    @pl.loop(0, count)
    def _(o):
        loads(o).start()

    barrier = pltpu.get_barrier_semaphore()

    def grid_peer(k):
        return lax.rem(grid_index + k, devices_grid)

    @pl.loop(1, devices_grid)
    def _(k):
        pl.semaphore_signal(barrier, inc=1, device_id={"grid": grid_peer(k)}, device_id_type=MESH)

    pl.semaphore_signal(barrier, inc=1, device_id={"band": 1 - band}, device_id_type=MESH)
    pl.semaphore_wait(barrier, devices_grid)

    can_send = []
    for dim in range(3):
        can_send += [pos[dim] < sizes[dim] - 1, pos[dim] > 0]
    can_recv = [can_send[1], can_send[0], can_send[3], can_send[2], can_send[5], can_send[4]]

    def face(stage, o, d):
        field = (xp, yp)[stage]
        if d == 0:
            src, dst = field.at[o, cx:cx + REACH, LEAD:LEAD + cy], field.at[o, 0:REACH, LEAD:LEAD + cy]
        elif d == 1:
            src = field.at[o, REACH:2 * REACH, LEAD:LEAD + cy]
            dst = field.at[o, cx + REACH:cx + 2 * REACH, LEAD:LEAD + cy]
        elif d < 4:
            src, dst = ypack.at[stage, o, d - 2], yrecv.at[stage, o, d - 2]
        else:
            src, dst = zpack.at[stage, o], zrecv.at[stage, o, d - 4]
        step = strides[d // 2] * (1 - 2 * (d % 2))
        return pltpu.make_async_remote_copy(
            src_ref=src, dst_ref=dst, send_sem=send_sem.at[stage, o, d], recv_sem=recv_sem.at[stage, o, d],
            device_id={"grid": grid_index + step}, device_id_type=MESH)

    for d in range(6):
        @pl.when(jnp.logical_not(can_recv[d]))
        def _(d=d):
            @pl.loop(0, 2 * count)
            def _(i):
                stage, o = i // count, i % count
                if d < 2:
                    start = (0, cx + REACH)[d]
                    for k in range(REACH):
                        zero = jnp.zeros((cy, cz), F32)

                        @pl.when(stage == 0)
                        def _():
                            xp[o, start + k, LEAD:LEAD + cy, :] = zero

                        @pl.when(stage == 1)
                        def _():
                            yp[o, start + k, LEAD:LEAD + cy, :] = zero
                elif d < 4:
                    yrecv[stage, o, d - 2] = jnp.zeros(yrecv.shape[3:], F32)
                else:
                    zrecv[stage, o, d - 4] = jnp.zeros(zrecv.shape[3:], F32)

    def pack_y(stage, field, o):
        for x in range(cx):
            ypack[stage, o, 0, REACH * x:REACH * (x + 1), :] = field[o, REACH + x, LEAD + cy - REACH:LEAD + cy, :]
            ypack[stage, o, 1, REACH * x:REACH * (x + 1), :] = field[o, REACH + x, LEAD:LEAD + REACH, :]

    def unpack_y(stage, field, o):
        for x in range(cx):
            field[o, REACH + x, LEAD - REACH:LEAD, :] = yrecv[stage, o, 0, REACH * x:REACH * (x + 1), :]
            field[o, REACH + x, LEAD + cy:LEAD + cy + REACH, :] = yrecv[stage, o, 1, REACH * x:REACH * (x + 1), :]

    lane = iota((8, cz), 1)
    lane_slot = lane // SLOT

    def pack_z_tile(stage, o, x0, y0, values):
        group, slot = x0 // per_pack, x0 % per_pack
        packed = zpack[stage, o, group, pl.ds(y0, 8), :]
        for u, value in enumerate(values):
            turned = pltpu.roll(value, (slot + u) * SLOT + REACH, 1)
            packed = jnp.where(lane_slot == slot + u, turned, packed)
        zpack[stage, o, group, pl.ds(y0, 8), :] = packed

    def correct_z(stage, o):
        own = zpack[stage, o]
        lanes = iota(own.shape, 2) % SLOT
        from_left = jnp.where(lanes < REACH, zrecv[stage, o, 0] - own, 0.0).reshape(-1, cz)
        right = (lanes >= REACH) & (lanes < 2 * REACH)
        from_right = jnp.where(right, zrecv[stage, o, 1] - own, 0.0).reshape(-1, cz)
        low_side, high_side = 0.0, 0.0
        for r in range(1, REACH + 1):
            low_side = low_side + TAPS[r] * pltpu.roll(from_left, r, 1)
            high_side = high_side + TAPS[r] * pltpu.roll(from_right, cz - r, 1)
        low_side, high_side = low_side.reshape(own.shape), high_side.reshape(own.shape)
        zcorr[...] = jnp.where(lanes < REACH, high_side, jnp.where(right, low_side, 0.0))

    edge = (lane < REACH) | (lane >= cz - REACH)

    def along_z(field, o, x0):
        start = field[o, pl.ds(x0 + REACH, UNROLL), LEAD:LEAD + cy, :].reshape(UNROLL * cy, cz)
        both = dot(jnp.concatenate(split(start), axis=1), band_z[...])
        return both[:, :cz] + both[:, cz:]

    def stencil_tile(field, o, x0, t, turned):
        y0 = 8 * t
        window = [field[o, x0 + i, LEAD + y0:LEAD + y0 + 8, :] for i in range(UNROLL + 2 * REACH)]
        results = []
        group, slot = x0 // per_pack, x0 % per_pack
        corr = zcorr[group, y0:y0 + 8, :]
        for u in range(UNROLL):
            center = window[u + REACH]
            total = pot[x0 + u, y0:y0 + 8, :] * center + turned[u * cy + y0:u * cy + y0 + 8]
            for r in range(1, REACH + 1):
                pair = window[u + REACH + r] + window[u + REACH - r]
                up = field[o, x0 + u + REACH, LEAD + y0 + r:LEAD + y0 + r + 8, :]
                down = field[o, x0 + u + REACH, LEAD + y0 - r:LEAD + y0 - r + 8, :]
                total = total + TAPS[r] * (pair + (up + down))
            fix = pltpu.roll(corr, cz - (slot + u) * SLOT - REACH, 1)
            results.append(total + jnp.where(edge, fix, 0.0))
        return results

    def start_faces(stage, o, sides=tuple(range(6))):
        for d in sides:
            @pl.when(can_send[d])
            def _(d=d):
                face(stage, o, d).start()

    def wait_faces(stage, o):
        for d in range(6):
            @pl.when(can_recv[d])
            def _(d=d):
                face(stage, o, d).wait_recv()

    @pl.loop(0, count)
    def _(o):
        loads(o).wait()
        start_faces(0, o, (0, 1))
        pack_y(0, xp, o)
        start_faces(0, o, (2, 3))

        @pl.loop(0, cx // UNROLL)
        def _(g):
            x0 = g * UNROLL
            for t in range(tiles):
                pack_z_tile(0, o, x0, 8 * t,
                            [xp[o, x0 + u + REACH, LEAD + 8 * t:LEAD + 8 * t + 8, :] for u in range(UNROLL)])

        start_faces(0, o, (4, 5))

    apart = jnp.abs(iota((cz, cz), 0) - iota((cz, cz), 1))
    weights = jnp.zeros((cz, cz), F32)
    for r in range(1, REACH + 1):
        weights = jnp.where((apart == r) | (apart == cz - r), TAPS[r], weights)
    weights_high, weights_low = split(weights)
    band_z[0:cz, 0:cz] = weights_high
    band_z[0:cz, cz:2 * cz] = weights_low
    band_z[cz:2 * cz, 0:cz] = weights_high
    band_z[cz:2 * cz, cz:2 * cz] = jnp.zeros((cz, cz), BF16)
    pot_load.wait()

    @pl.loop(0, cx)
    def _(x):
        pot[x] = (pot[x] + DIAGONAL) * (1.0 / HALF_WIDTH)

    @pl.loop(0, count)
    def _(o):
        wait_faces(0, o)
        unpack_y(0, xp, o)
        correct_z(0, o)

        @pl.loop(0, cx // UNROLL)
        def _(g):
            x0 = g * UNROLL
            turned = along_z(xp, o, x0)
            for t in range(tiles):
                values = stencil_tile(xp, o, x0, t, turned)
                for u in range(UNROLL):
                    yp[o, x0 + u + REACH, LEAD + 8 * t:LEAD + 8 * t + 8, :] = values[u]
                pack_z_tile(1, o, x0, 8 * t, values)

        start_faces(1, o, (0, 1, 4, 5))
        pack_y(1, yp, o)
        start_faces(1, o, (2, 3))

    def hand_over(o):
        return pltpu.make_async_remote_copy(
            src_ref=y2.at[o], dst_ref=rem.at[o], send_sem=y2_send.at[o], recv_sem=y2_recv.at[o],
            device_id={"band": 1 - band}, device_id_type=MESH)

    @pl.loop(0, count)
    def _(o):
        wait_faces(1, o)
        unpack_y(1, yp, o)
        correct_z(1, o)

        @pl.loop(0, cx // UNROLL)
        def _(g):
            x0 = g * UNROLL
            turned = along_z(yp, o, x0)
            for t in range(tiles):
                values = stencil_tile(yp, o, x0, t, turned)
                for u in range(UNROLL):
                    start = xp[o, x0 + u + REACH, LEAD + 8 * t:LEAD + 8 * t + 8, :]
                    y2[o, x0 + u, 8 * t:8 * t + 8, :] = (values[u] + values[u]) - start

        hand_over(o).start()

    def wide(ref, x0):
        return jnp.concatenate([ref[:, x0 + u].reshape(rows, cz) for u in range(UNROLL)], axis=1)

    def split_block(which, field, x0):
        for u in range(UNROLL):
            high[which, :, x0 + u], low[which, :, x0 + u] = split(field[:, x0 + u])

    def gram(which):
        acc[...] = jnp.zeros_like(acc)

        @pl.loop(0, cx // UNROLL)
        def _(g):
            x0 = g * UNROLL
            split_block(which, (y2, rem)[which], x0)
            left_high, left_low = wide(high.at[0], x0), wide(low.at[0], x0)
            right_high, right_low = wide(high.at[which], x0), wide(low.at[which], x0)
            inner = ((1,), (1,))
            acc[...] += dot(jnp.concatenate([left_high, left_high, left_low], axis=1),
                            jnp.concatenate([right_high, right_low, right_high], axis=1), inner)

    same_y = (iota((rows, rows), 0) % cy) == (iota((rows, rows), 1) % cy)

    def row_pick(which):
        own = jnp.where(which == 0, band, 1 - band) * count
        return (iota((2 * count, rows), 0) == iota((2 * count, rows), 1) // cy + own).astype(F32)

    def column_pick(which):
        own = jnp.where(which == 0, band, 1 - band) * count
        return (iota((rows, cz), 1) == iota((rows, cz), 0) // cy + own).astype(F32)

    gram(0)
    masked = jnp.where(same_y, acc[...], 0.0)
    place[0] = dot(dot(row_pick(0), masked, precision=HIGHEST), column_pick(0), precision=HIGHEST)
    oo_copy = pltpu.make_async_remote_copy(
        src_ref=place.at[0], dst_ref=place.at[1], send_sem=oo_send, recv_sem=oo_recv,
        device_id={"band": 1 - band}, device_id_type=MESH)
    oo_copy.start()

    @pl.loop(0, count)
    def _(o):
        hand_over(o).wait_recv()

    gram(1)
    masked = jnp.where(same_y, acc[...], 0.0)
    cross = dot(dot(row_pick(0), masked, precision=HIGHEST), column_pick(1), precision=HIGHEST)
    flipped = dot(dot(row_pick(1), masked, ((1,), (1,)), HIGHEST), column_pick(0), precision=HIGHEST)
    oo_copy.wait_recv()
    total = place[0] + place[1] + cross + flipped

    sums[grid_index] = total

    def reduce_copy(k):
        return pltpu.make_async_remote_copy(
            src_ref=sums.at[grid_index], dst_ref=sums.at[grid_index],
            send_sem=ar_send.at[k], recv_sem=ar_recv.at[k],
            device_id={"grid": grid_peer(k)}, device_id_type=MESH)

    @pl.loop(1, devices_grid)
    def _(k):
        reduce_copy(k).start()

    @pl.loop(1, devices_grid)
    def _(k):
        reduce_copy(k).wait_recv()

    total = sums[0]
    for k in range(1, devices_grid):
        total = total + sums[k]

    orbs = 2 * count
    row_id, lane_id = iota((orbs, cz), 0), iota((orbs, cz), 1)
    work = jnp.where(lane_id < orbs, total * (1.0 / volume), (lane_id == row_id + orbs).astype(F32))
    for k in range(orbs):
        scale = 1.0 / jnp.sqrt(work[k:k + 1, k:k + 1])
        pivot = work[k:k + 1, :] * scale
        column = jnp.where(row_id > k, work[:, k:k + 1] * scale, 0.0)
        work = jnp.where(row_id == k, pivot, work - column * pivot)

    def spread(which):
        own = jnp.where(which == 0, band, 1 - band) * count
        rows_pick = (iota((rows, orbs), 1) == iota((rows, orbs), 0) // cy + band * count).astype(F32)
        lanes_pick = (iota((cz, rows), 0) == iota((cz, rows), 1) // cy + own + orbs).astype(F32)
        full = dot(dot(rows_pick, work, precision=HIGHEST), lanes_pick, precision=HIGHEST)
        return split(jnp.where(same_y, full, 0.0))

    own_high, own_low = spread(0)
    far_high, far_low = spread(1)

    def store(x0):
        return pltpu.make_async_copy(
            outv.at[:, pl.ds(x0, UNROLL)], out_hbm.at[0, :, pl.ds(x0, UNROLL)], out_sem.at[x0 // UNROLL])

    @pl.loop(0, cx // UNROLL)
    def _(g):
        x0 = g * UNROLL
        a_high, a_low = wide(high.at[0], x0), wide(low.at[0], x0)
        b_high, b_low = wide(high.at[1], x0), wide(low.at[1], x0)
        result = (dot(own_high, a_high) + dot(own_high, a_low) + dot(own_low, a_high)
                  + dot(far_high, b_high) + dot(far_high, b_low) + dot(far_low, b_high))
        for u in range(UNROLL):
            outv[:, x0 + u] = result[:, u * cz:(u + 1) * cz].reshape(count, cy, cz)
        store(x0).start()

    @pl.loop(0, cx // UNROLL)
    def _(g):
        store(g * UNROLL).wait()

    @pl.loop(0, count)
    def _(o):
        for stage in range(2):
            for d in range(6):
                @pl.when(can_send[d])
                def _(stage=stage, d=d):
                    face(stage, o, d).wait_send()
        hand_over(o).wait_send()

    oo_copy.wait_send()

    @pl.loop(1, devices_grid)
    def _(k):
        reduce_copy(k).wait_send()


def on_device(orbitals, potential):
    _, count, cx, cy, cz = orbitals.shape
    devices_grid = lax.axis_size("grid")
    parts = layout(devices_grid)
    volume = cx * cy * cz * devices_grid
    rows, orbs = count * cy, 2 * count
    groups = cx * SLOT // cz
    padded = (count, cx + 2 * REACH, cy + 2 * LEAD, cz)
    block = (count, cx, cy, cz)
    dma = pltpu.SemaphoreType.DMA
    any_spec = pl.BlockSpec(memory_space=pl.ANY)
    return pl.pallas_call(
        functools.partial(kernel, parts, volume),
        out_shape=jax.ShapeDtypeStruct(orbitals.shape, F32),
        in_specs=[any_spec, any_spec],
        out_specs=any_spec,
        scratch_shapes=[
            pltpu.VMEM(padded, F32), pltpu.VMEM(padded, F32),
            pltpu.VMEM(block, F32), pltpu.VMEM(block, F32), pltpu.VMEM((cx, cy, cz), F32),
            pltpu.VMEM((2, count, 2, REACH * cx, cz), F32), pltpu.VMEM((2, count, 2, REACH * cx, cz), F32),
            pltpu.VMEM((2, count, groups, cy, cz), F32), pltpu.VMEM((2, count, 2, groups, cy, cz), F32),
            pltpu.VMEM((groups, cy, cz), F32),
            pltpu.VMEM((2,) + block, BF16), pltpu.VMEM((2,) + block, BF16),
            pltpu.VMEM((rows, rows), F32), pltpu.VMEM((2, orbs, cz), F32),
            pltpu.VMEM((devices_grid, orbs, cz), F32), pltpu.VMEM((2 * cz, 2 * cz), BF16),
            pltpu.VMEM(block, F32),
            dma((count + 1,)), dma((2, count, 6)), dma((2, count, 6)), dma((count,)), dma((count,)),
            dma, dma, dma((devices_grid,)), dma((devices_grid,)), dma((cx // UNROLL,)),
        ],
        compiler_params=pltpu.CompilerParams(
            collective_id=0, has_side_effects=True, vmem_limit_bytes=60 * 1024 * 1024),
    )(orbitals, potential)


def solution(mesh):
    in_specs = (P("grid", "band", None, None, None), P("grid", None, None, None))
    out_specs = P("grid", "band", None, None, None)
    return jax.shard_map(
        on_device, mesh=mesh, in_specs=in_specs, out_specs=out_specs, check_vma=False
    )
```
